32 devices in a mesh: rows: 2 (over x), feat: 16 (over z, y, core).
Axes of the slice: x: 2, y: 2, z: 4, core: 2. Of those that a mesh axis runs over, the one named last changes fastest.
Arguments:
- slab_grads: bfloat16 [448, 262144], P('rows', 'feat'), may hold values from -6 to 6
- basis: bfloat16 [262144, 1024], P('feat', 'rows'), may hold values from -0.01171875 to 0.01171875
- eigenvalues: float32 [1024], replicated, may hold values from 0.02 to 2
- store_rows: bfloat16 [16384, 1024], P(('rows', 'feat')), may hold values from -0.1875 to 0.1875
- slab_index: int32 [448], replicated, may hold values from 0 to 16383
Outputs:
- scores: float32 [448, 16384], P(None, ('rows', 'feat'))
The draws below stay inside these ranges and needn't reach their ends.
All inputs are finite; a program needn't handle non-finite values.
Results may differ from the reference program's by a relative error of at most 0.0029.
Values may be sent and summed in bfloat16 or wider, within the bound.
No kernel may reach another device: no remote copies, remote signals or barrier semaphores. Data moves between devices by JAX's collectives and lax.ppermute only.
A program may use at most 128 MiB of HBM per device.

```python
import math
import jax
import jax.numpy as jnp
from jax import lax

F = 262144
K = 1024
S = 448
N = 16384


def plant(result, key, low, high):
    longest = result.shape.index(max(result.shape))
    spots = []
    for shift in (0, 1):
        where = [jax.random.randint(jax.random.fold_in(key, axis), (), 0, length) for axis, length in enumerate(result.shape)]
        where[longest] = (where[longest] + shift) % result.shape[longest]
        spots.append(tuple(where))
    return result.at[spots[0]].set(low).at[spots[1]].set(high)


def shard_levels(key, dims, cuts, smallest, top_value):
    def one(dim, shards_of):
        steps = jax.random.uniform(jax.random.fold_in(jax.random.fold_in(key, 6), dim), (shards_of,), jnp.float32, smallest / len(cuts), top_value / len(cuts))
        return jnp.repeat(jnp.exp(steps), dims[dim] // shards_of).reshape((-1,) + (1,) * (len(dims) - dim - 1))

    level = one(*cuts[0])
    for cut in cuts[1:]:
        level = level * one(*cut)
    return level


def bell_draw(own_key, dims, deviation, reach, shards=(), kind=jnp.bfloat16):
    values = deviation * jax.random.normal(own_key, dims, jnp.float32)
    if shards:
        values = values * shard_levels(own_key, dims, shards, -0.22, 0.18)
    return jnp.clip(values, -reach, reach).astype(kind)


def setup_inputs(seed: int = 0) -> dict:
    arg_keys = jax.random.split(jax.random.key(seed), 6)
    slab_grads = bell_draw(arg_keys[0], (S, F), 1.0, 6.0, ((0, 2), (1, 16)))
    basis = bell_draw(arg_keys[1], (F, K), F ** -0.5, 0.01171875, ((0, 16), (1, 2)))
    eigenvalues = jnp.clip(jnp.exp(jax.random.uniform(arg_keys[2], (K,), jnp.float32, math.log(0.02), math.log(2.0))), 0.02, 2.0)
    store_rows = bell_draw(arg_keys[3], (N, K), K ** -0.5, 0.1875, ((0, 32),))
    slab_index = plant(jax.random.randint(arg_keys[4], (S,), 0, N), jax.random.fold_in(arg_keys[4], 1), 0, N - 1).astype(jnp.int32)
    return {"slab_grads": slab_grads, "basis": basis, "eigenvalues": eigenvalues, "store_rows": store_rows, "slab_index": slab_index}


DAMPING = 0.1


def reference(slab_grads, basis, eigenvalues, store_rows, slab_index):
    feature_block = min(F, 8192)
    block_count = F // feature_block

    def advance(number, running):
        offset = (number * feature_block).astype(jnp.int32)
        grads_block = lax.dynamic_slice_in_dim(slab_grads, offset, feature_block, 1).astype(jnp.float32)
        basis_block = lax.dynamic_slice_in_dim(basis, offset, feature_block, 0).astype(jnp.float32)
        return running + jnp.dot(grads_block, basis_block, preferred_element_type=jnp.float32)

    projection = lax.fori_loop(0, block_count, advance, jnp.zeros((S, K), jnp.float32))
    whitened = (projection / (eigenvalues + DAMPING)).astype(jnp.bfloat16)
    product = lax.dot_general(whitened, store_rows, (((1,), (1,)), ((), ())), preferred_element_type=jnp.float32)
    columns = jnp.arange(N, dtype=jnp.int32)
    return jnp.where(slab_index[:, None] == columns[None, :], jnp.zeros_like(product), product)
```

```python
import functools

import jax
import jax.numpy as jnp
from jax import lax
from jax.experimental import pallas as pl
from jax.experimental.pallas import tpu as pltpu
from jax.sharding import PartitionSpec as P


DAMPING = 0.1
CONTRACT_LAST = (((1,), (1,)), ((), ()))


def parity(number, count):
    bits = 0
    while count > 1:
        bits = bits ^ number
        number = number >> 1
        count //= 2
    return bits & 1


def exchange(value, row_groups, feat_groups, row_flip, feat_flip):
    count = row_groups * feat_groups
    pairs = [
        (i, (((i // feat_groups) ^ row_flip) * feat_groups) + ((i % feat_groups) ^ feat_flip))
        for i in range(count)
    ]
    return lax.ppermute(value, ("rows", "feat"), pairs)


def after(value, *needed):
    return lax.optimization_barrier((value, *needed))[0]


def score_kernel(where_ref, whitened_ref, store_ref, index_ref, out_ref):
    product = lax.dot_general(
        whitened_ref[...], store_ref[...], CONTRACT_LAST, preferred_element_type=jnp.float32
    )
    columns = where_ref[1] + lax.broadcasted_iota(jnp.int32, product.shape, 1)
    out_ref[...] = jnp.where(index_ref[...] == columns, jnp.zeros_like(product), product)


def score(whitened, store, slab_index, row, first_column, row_groups):
    rows = whitened.shape[0] // row_groups
    directions = whitened.shape[1]
    count = store.shape[0]
    return pl.pallas_call(
        score_kernel,
        out_shape=jax.ShapeDtypeStruct((whitened.shape[0], count), jnp.float32),
        grid_spec=pltpu.PrefetchScalarGridSpec(
            num_scalar_prefetch=1,
            grid=(row_groups,),
            in_specs=[
                pl.BlockSpec((rows, directions), lambda a, where: (a, 0)),
                pl.BlockSpec((count, directions), lambda a, where: (0, 0)),
                pl.BlockSpec((rows, 1), lambda a, where: (a ^ where[0], 0)),
            ],
            out_specs=pl.BlockSpec((rows, count), lambda a, where: (a ^ where[0], 0)),
        ),
        name="score",
    )(jnp.stack([row, first_column]).astype(jnp.int32), whitened, store, slab_index[:, None])


def shards(slab_grads, basis, eigenvalues, store_rows, slab_index, *, row_groups, feat_groups):
    row, feat = lax.axis_index("rows"), lax.axis_index("feat")
    store_count = store_rows.shape[0]
    first_column = (row * feat_groups + feat) * store_count
    rows, features = slab_grads.shape
    directions = basis.shape[1]
    half = directions // 2
    side = parity(row, row_groups) ^ parity(feat, feat_groups)
    swap = functools.partial(exchange, row_groups=row_groups, feat_groups=feat_groups)

    def cross(value, flip):
        return swap(value, row_flip=flip, feat_flip=bin(flip).count("1") & 1)

    tail = max(rows * 3 // 14 // 16 * 16, 16)
    lead = 16
    middle = lead + (rows - tail - lead) // 16 * 8
    cuts = [0, lead, middle, rows - tail]
    feature_cuts = [0, features // 2, features * 7 // 8, features]

    last = row_groups - 1
    far = [swap(slab_grads, row_flip=flip, feat_flip=0) for flip in range(1, last)]
    head = slab_grads[:lead]
    rest = after(slab_grads, head)
    pieces = [head] + [rest[a:b] for a, b in zip(cuts[1:-1], cuts[2:])]
    pieces += [rest[rows - tail :, a:b] for a, b in zip(feature_cuts[:-1], feature_cuts[1:])]
    moved = []
    for piece in pieces:
        moved.append(swap(piece, row_flip=last, feat_flip=0))

    scales = lax.dynamic_slice_in_dim(
        eigenvalues, row * directions + side * half, half, 0
    )[None, :] + DAMPING
    order = []
    for flip in range(row_groups):
        base = (row ^ flip) * directions
        for part in (side, 1 - side):
            order.append(lax.dynamic_slice_in_dim(store_rows, base + part * half, half, 1))
    store = jnp.concatenate(order, 1)

    def project(block, a=0, b=features):
        return jnp.dot(block, basis[a:b], preferred_element_type=jnp.float32)

    def halves(partial_value):
        mine = lax.dynamic_slice_in_dim(partial_value, side * half, half, 1)
        other = lax.dynamic_slice_in_dim(partial_value, (1 - side) * half, half, 1)
        return mine + swap(other, row_flip=0, feat_flip=1)

    def totals(total):
        yield total
        bit = 2
        while bit < feat_groups:
            total = total + swap(total, row_flip=0, feat_flip=bit | 1)
            bit *= 2
            yield total

    def whiten(total):
        return (total / scales).astype(jnp.bfloat16)

    def reduce(partial_value):
        return whiten(list(totals(halves(partial_value)))[-1])

    early = [reduce(project(after(slab_grads, *pieces)))]
    for block in far:
        early.append(reduce(project(after(block, early[-1]))))
    first, second, third = moved[:3]
    lead_value = project(after(first, early[-1]))
    near = project(after(second, early[-1], lead_value))
    early.append(reduce(jnp.concatenate([lead_value, near], 0)))
    middle = project(after(third, early[-1]))
    middle_totals = list(totals(halves(middle)))
    early.append(whiten(middle_totals[-1]))
    early = jnp.concatenate(early, 0)
    early = jnp.concatenate([early, swap(early, row_flip=0, feat_flip=1)], 1)
    early = [early] + [cross(early, flip) for flip in range(1, row_groups)]

    late = project(after(moved[3], middle_totals[1]), *feature_cuts[:2])
    late += project(after(moved[4], late, middle_totals[2]), *feature_cuts[1:3])
    late += project(after(moved[5], late, early[0]), *feature_cuts[2:])
    late = reduce(late)
    late = jnp.concatenate([late] + [cross(late, flip) for flip in range(1, row_groups)], 0)
    pair = swap(late, row_flip=0, feat_flip=1)
    late = [
        jnp.concatenate([late[f * tail : (f + 1) * tail], pair[f * tail : (f + 1) * tail]], 1)
        for f in range(row_groups)
    ]
    columns = []
    for flip in range(row_groups):
        whole = jnp.concatenate([early[flip], late[flip]], 0)
        order = [a ^ flip for a in range(row_groups)]
        columns.append(
            whole
            if flip == 0
            else jnp.concatenate([whole[i * rows : (i + 1) * rows] for i in order], 0)
        )
    whitened = jnp.concatenate(columns, 1)
    return score(whitened, store, slab_index, row, first_column, row_groups)


def plain(slab_grads, basis, eigenvalues, store_rows, slab_index, *, row_groups, feat_groups):
    store_count = store_rows.shape[0]
    first_column = (lax.axis_index("rows") * feat_groups + lax.axis_index("feat")) * store_count
    columns = first_column + jnp.arange(store_count, dtype=jnp.int32)
    local_dirs = basis.shape[1]
    partial_value = jnp.dot(
        lax.all_gather(slab_grads, "rows", axis=0, tiled=True),
        basis,
        preferred_element_type=jnp.float32,
    )
    summed = lax.psum(partial_value, "feat")
    scales = lax.dynamic_slice_in_dim(
        eigenvalues, lax.axis_index("rows") * local_dirs, local_dirs, 0
    )
    whitened = (summed / (scales + DAMPING)).astype(jnp.bfloat16)
    gathered = lax.all_gather(whitened, "rows", axis=1, tiled=True)
    product = lax.dot_general(
        gathered, store_rows, CONTRACT_LAST, preferred_element_type=jnp.float32
    )
    return jnp.where(slab_index[:, None] == columns[None, :], jnp.zeros_like(product), product)


def solution(mesh):
    row_groups, feat_groups = mesh.shape["rows"], mesh.shape["feat"]
    powers = all(n > 1 and n & (n - 1) == 0 for n in (row_groups, feat_groups))

    def body(*args):
        sizes = dict(row_groups=row_groups, feat_groups=feat_groups)
        rows = args[0].shape[0]
        if not powers or rows < 96 or rows % 16 or args[1].shape[1] % 2:
            return plain(*args, **sizes)
        return shards(*args, **sizes)

    in_specs = (P("rows", "feat"), P("feat", "rows"), P(), P(("rows", "feat"), None), P())
    out_specs = P(None, ("rows", "feat"))
    return jax.shard_map(body, mesh=mesh, in_specs=in_specs, out_specs=out_specs, check_vma=False)
```

```python
import functools

import jax
import jax.numpy as jnp
from jax import lax
from jax.experimental import pallas as pl
from jax.experimental.pallas import tpu as pltpu
from jax.sharding import PartitionSpec as P


DAMPING = 0.1
CONTRACT_LAST = (((1,), (1,)), ((), ()))


def parity(number, count):
    bits = 0
    while count > 1:
        bits = bits ^ number
        number = number >> 1
        count //= 2
    return bits & 1


def exchange(value, row_groups, feat_groups, row_flip, feat_flip):
    count = row_groups * feat_groups
    pairs = [
        (i, (((i // feat_groups) ^ row_flip) * feat_groups) + ((i % feat_groups) ^ feat_flip))
        for i in range(count)
    ]
    return lax.ppermute(value, ("rows", "feat"), pairs)


def after(value, *needed):
    return lax.optimization_barrier((value, *needed))[0]


def score_kernel(row_groups, rows, tail, _, *refs):
    early = refs[:row_groups]
    late_ref, pair_ref, store_ref, index_ref, out_ref = refs[row_groups:]
    half = late_ref.shape[1]
    same = index_ref[...] == lax.broadcasted_iota(jnp.int32, out_ref.shape, 1)

    def dot(block, flip, part, size):
        spot = (2 * flip + part) * half
        return lax.dot_general(
            block,
            store_ref[:, spot : spot + size],
            CONTRACT_LAST,
            preferred_element_type=jnp.float32,
        )

    for place in range(row_groups):

        @pl.when(pl.program_id(0) == place)
        def _():
            head, foot = 0.0, 0.0
            for flip in range(row_groups):
                block = (place ^ flip) * rows
                head += dot(early[flip][block : block + rows - tail, :], flip, 0, 2 * half)
                if place ^ flip == row_groups - 1:
                    spot = flip * tail
                    foot += dot(late_ref[spot : spot + tail, :], flip, 0, half)
                    foot += dot(pair_ref[spot : spot + tail, :], flip, 1, half)
                else:
                    foot += dot(
                        early[flip][block + rows - tail : block + rows, :], flip, 0, 2 * half
                    )
            product = jnp.concatenate([head, foot], 0)
            out_ref[...] = jnp.where(same, jnp.zeros_like(product), product)


def score(where, early, late, pair, store, slab_index, rows, tail):
    row_groups, count = len(early), store.shape[0]
    whole = [
        pl.BlockSpec(a.shape, lambda a, where: (0, 0)) for a in (*early, late, pair, store)
    ]
    return pl.pallas_call(
        functools.partial(score_kernel, row_groups, rows, tail),
        out_shape=jax.ShapeDtypeStruct((rows * row_groups, count), jnp.float32),
        grid_spec=pltpu.PrefetchScalarGridSpec(
            num_scalar_prefetch=1,
            grid=(row_groups,),
            in_specs=whole + [pl.BlockSpec((rows, 1), lambda a, where: (a ^ where[0], 0))],
            out_specs=pl.BlockSpec((rows, count), lambda a, where: (a ^ where[0], 0)),
        ),
        compiler_params=pltpu.CompilerParams(vmem_limit_bytes=24 << 20),
        name="score",
    )(where, *early, late, pair, store, slab_index)


def shards(slab_grads, basis, eigenvalues, store_rows, slab_index, *, row_groups, feat_groups):
    row, feat = lax.axis_index("rows"), lax.axis_index("feat")
    store_count = store_rows.shape[0]
    first_column = (row * feat_groups + feat) * store_count
    rows, features = slab_grads.shape
    directions = basis.shape[1]
    half = directions // 2
    side = parity(row, row_groups) ^ parity(feat, feat_groups)
    swap = functools.partial(exchange, row_groups=row_groups, feat_groups=feat_groups)

    def cross(value, flip):
        return swap(value, row_flip=flip, feat_flip=bin(flip).count("1") & 1)

    tail = max(rows // 7 // 16 * 16, 16)
    near = (rows - tail) * 2 // 3 // 16 * 16
    lead = min(32, near // 2)
    quarter = features // 4
    cuts = [
        (0, lead, 0, quarter),
        (0, lead, quarter, features),
        (lead, near, 0, features),
        (near, rows - tail, 0, features),
        (rows - tail, rows, 0, 2 * quarter),
        (rows - tail, rows, 2 * quarter, features - quarter // 2),
        (rows - tail, rows, features - quarter // 2, features),
    ]

    last = row_groups - 1
    far = [swap(slab_grads, row_flip=flip, feat_flip=0) for flip in range(1, last)]
    pieces, ready = [], slab_grads
    for i, (r0, r1, f0, f1) in enumerate(cuts):
        pieces.append(ready[r0:r1, f0:f1])
        if i < 2:
            ready = after(slab_grads, pieces[-1])
    moved = []
    for piece in pieces:
        moved.append(swap(piece, row_flip=last, feat_flip=0))

    scales = lax.dynamic_slice_in_dim(
        eigenvalues, row * directions + side * half, half, 0
    )[None, :] + DAMPING
    order = []
    for flip in range(row_groups):
        base = (row ^ flip) * directions
        for part in (side, 1 - side):
            order.append(lax.dynamic_slice_in_dim(store_rows, base + part * half, half, 1))
    store = jnp.concatenate(order, 1)
    where = row.astype(jnp.int32).reshape(1)
    index = slab_index[:, None] - first_column

    def project(i, *needed):
        _, _, f0, f1 = cuts[i]
        return jnp.dot(
            after(moved[i], *needed), basis[f0:f1], preferred_element_type=jnp.float32
        )

    def halves(partial_value):
        mine = lax.dynamic_slice_in_dim(partial_value, side * half, half, 1)
        other = lax.dynamic_slice_in_dim(partial_value, (1 - side) * half, half, 1)
        return mine + swap(other, row_flip=0, feat_flip=1)

    def totals(total):
        yield total
        bit = 2
        while bit < feat_groups:
            total = total + swap(total, row_flip=0, feat_flip=bit | 1)
            bit *= 2
            yield total

    def whiten(total):
        return (total / scales).astype(jnp.bfloat16)

    def reduce(partial_value):
        return whiten(list(totals(halves(partial_value)))[-1])

    blocks = [after(slab_grads, *pieces)] + far
    early = []
    for block in blocks:
        early.append(
            reduce(jnp.dot(after(block, *early), basis, preferred_element_type=jnp.float32))
        )
    first = project(0, early[-1], store, where, index)
    first += project(1, first)
    early.append(reduce(jnp.concatenate([first, project(2, first)], 0)))
    middle = project(3, early[-1])
    middle_totals = list(totals(halves(middle)))
    early.append(whiten(middle_totals[-1]))
    early = jnp.concatenate(early, 0)
    early = jnp.concatenate([early, swap(early, row_flip=0, feat_flip=1)], 1)
    early = [early] + [cross(early, flip) for flip in range(1, row_groups)]

    late = project(4, middle_totals[1])
    late += project(5, late, early[0])
    late += project(6, late)
    late = reduce(late)
    late = jnp.concatenate([late] + [cross(late, flip) for flip in range(1, row_groups)], 0)
    pair = swap(late, row_flip=0, feat_flip=1)
    return score(where, early, late, pair, store, index, rows, tail)


def plain(slab_grads, basis, eigenvalues, store_rows, slab_index, *, row_groups, feat_groups):
    store_count = store_rows.shape[0]
    first_column = (lax.axis_index("rows") * feat_groups + lax.axis_index("feat")) * store_count
    columns = first_column + jnp.arange(store_count, dtype=jnp.int32)
    local_dirs = basis.shape[1]
    partial_value = jnp.dot(
        lax.all_gather(slab_grads, "rows", axis=0, tiled=True),
        basis,
        preferred_element_type=jnp.float32,
    )
    summed = lax.psum(partial_value, "feat")
    scales = lax.dynamic_slice_in_dim(
        eigenvalues, lax.axis_index("rows") * local_dirs, local_dirs, 0
    )
    whitened = (summed / (scales + DAMPING)).astype(jnp.bfloat16)
    gathered = lax.all_gather(whitened, "rows", axis=1, tiled=True)
    product = lax.dot_general(
        gathered, store_rows, CONTRACT_LAST, preferred_element_type=jnp.float32
    )
    return jnp.where(slab_index[:, None] == columns[None, :], jnp.zeros_like(product), product)


def solution(mesh):
    row_groups, feat_groups = mesh.shape["rows"], mesh.shape["feat"]
    powers = all(n > 1 and n & (n - 1) == 0 for n in (row_groups, feat_groups))

    def body(*args):
        sizes = dict(row_groups=row_groups, feat_groups=feat_groups)
        rows = args[0].shape[0]
        if not powers or rows < 96 or rows % 16 or args[1].shape[1] % 2:
            return plain(*args, **sizes)
        return shards(*args, **sizes)

    in_specs = (P("rows", "feat"), P("feat", "rows"), P(), P(("rows", "feat"), None), P())
    out_specs = P(None, ("rows", "feat"))
    return jax.shard_map(body, mesh=mesh, in_specs=in_specs, out_specs=out_specs, check_vma=False)
```

```python
import functools

import jax
import jax.numpy as jnp
from jax import lax
from jax.experimental import pallas as pl
from jax.experimental.pallas import tpu as pltpu
from jax.sharding import PartitionSpec as P


DAMPING = 0.1
CONTRACT_LAST = (((1,), (1,)), ((), ()))


def parity(number, count):
    bits = 0
    while count > 1:
        bits = bits ^ number
        number = number >> 1
        count //= 2
    return bits & 1


def exchange(value, row_groups, feat_groups, row_flip, feat_flip):
    count = row_groups * feat_groups
    pairs = [
        (i, (((i // feat_groups) ^ row_flip) * feat_groups) + ((i % feat_groups) ^ feat_flip))
        for i in range(count)
    ]
    return lax.ppermute(value, ("rows", "feat"), pairs)


def after(value, *needed):
    return lax.optimization_barrier((value, *needed))[0]


def score_kernel(row_groups, rows, tail, _, *refs):
    early = refs[:row_groups]
    late_ref, pair_ref, store_ref, index_ref, out_ref = refs[row_groups:]
    half = late_ref.shape[1]
    same = index_ref[...] == lax.broadcasted_iota(jnp.int32, out_ref.shape, 1)

    def dot(block, flip, part, size):
        spot = (2 * flip + part) * half
        return lax.dot_general(
            block,
            store_ref[:, spot : spot + size],
            CONTRACT_LAST,
            preferred_element_type=jnp.float32,
        )

    for place in range(row_groups):

        @pl.when(pl.program_id(0) == place)
        def _():
            head, foot = 0.0, 0.0
            for flip in range(row_groups):
                block = (place ^ flip) * rows
                head += dot(early[flip][block : block + rows - tail, :], flip, 0, 2 * half)
                if place ^ flip == row_groups - 1:
                    spot = flip * tail
                    foot += dot(late_ref[spot : spot + tail, :], flip, 0, half)
                    foot += dot(pair_ref[spot : spot + tail, :], flip, 1, half)
                else:
                    foot += dot(
                        early[flip][block + rows - tail : block + rows, :], flip, 0, 2 * half
                    )
            product = jnp.concatenate([head, foot], 0)
            out_ref[...] = jnp.where(same, jnp.zeros_like(product), product)


def score(where, early, late, pair, store, slab_index, rows, tail):
    row_groups, count = len(early), store.shape[0]
    whole = [
        pl.BlockSpec(a.shape, lambda a, where: (0, 0)) for a in (*early, late, pair, store)
    ]
    return pl.pallas_call(
        functools.partial(score_kernel, row_groups, rows, tail),
        out_shape=jax.ShapeDtypeStruct((rows * row_groups, count), jnp.float32),
        grid_spec=pltpu.PrefetchScalarGridSpec(
            num_scalar_prefetch=1,
            grid=(row_groups,),
            in_specs=whole + [pl.BlockSpec((rows, 1), lambda a, where: (a ^ where[0], 0))],
            out_specs=pl.BlockSpec((rows, count), lambda a, where: (a ^ where[0], 0)),
        ),
        compiler_params=pltpu.CompilerParams(vmem_limit_bytes=24 << 20),
        name="score",
    )(where, *early, late, pair, store, slab_index)


def shards(slab_grads, basis, eigenvalues, store_rows, slab_index, *, row_groups, feat_groups):
    row, feat = lax.axis_index("rows"), lax.axis_index("feat")
    store_count = store_rows.shape[0]
    first_column = (row * feat_groups + feat) * store_count
    rows, features = slab_grads.shape
    directions = basis.shape[1]
    half = directions // 2
    side = parity(row, row_groups) ^ parity(feat, feat_groups)
    swap = functools.partial(exchange, row_groups=row_groups, feat_groups=feat_groups)

    def cross(value, flip):
        return swap(value, row_flip=flip, feat_flip=bin(flip).count("1") & 1)

    tail = max(rows // 7 // 16 * 16, 16)
    near = (rows - tail) * 2 // 3 // 16 * 16
    lead = min(32, near // 2)
    quarter = features // 4
    cuts = [
        (0, lead, 0, quarter),
        (0, lead, quarter, features),
        (lead, near, 0, features),
        (near, rows - tail, 0, features),
        (rows - tail, rows, 0, 2 * quarter),
        (rows - tail, rows, 2 * quarter, features - quarter // 2),
        (rows - tail, rows, features - quarter // 2, features),
    ]

    last = row_groups - 1
    far = [swap(slab_grads, row_flip=flip, feat_flip=0) for flip in range(1, last)]
    pieces, ready = [], slab_grads
    for i, (r0, r1, f0, f1) in enumerate(cuts):
        pieces.append(ready[r0:r1, f0:f1])
        if i < 2:
            ready = after(slab_grads, pieces[-1])
    moved = []
    for piece in pieces:
        moved.append(swap(piece, row_flip=last, feat_flip=0))

    scales = lax.dynamic_slice_in_dim(
        eigenvalues, row * directions + side * half, half, 0
    )[None, :] + DAMPING
    order = []
    for flip in range(row_groups):
        base = (row ^ flip) * directions
        for part in (side, 1 - side):
            order.append(lax.dynamic_slice_in_dim(store_rows, base + part * half, half, 1))
    store = jnp.concatenate(order, 1)
    where = row.astype(jnp.int32).reshape(1)
    index = slab_index[:, None] - first_column

    def project(i, *needed):
        _, _, f0, f1 = cuts[i]
        return jnp.dot(
            after(moved[i], *needed), basis[f0:f1], preferred_element_type=jnp.float32
        )

    def halves(partial_value):
        mine = lax.dynamic_slice_in_dim(partial_value, side * half, half, 1)
        other = lax.dynamic_slice_in_dim(partial_value, (1 - side) * half, half, 1)
        return mine + swap(other, row_flip=0, feat_flip=1)

    def totals(total):
        yield total
        bit = 2
        while bit < feat_groups:
            total = total + swap(total, row_flip=0, feat_flip=bit | 1)
            bit *= 2
            yield total

    def whiten(total):
        return (total / scales).astype(jnp.bfloat16)

    def reduce(partial_value):
        return whiten(list(totals(halves(partial_value)))[-1])

    blocks = [after(slab_grads, *pieces)] + far
    early = []
    for block in blocks:
        early.append(
            reduce(jnp.dot(after(block, *early), basis, preferred_element_type=jnp.float32))
        )
    first = project(0, early[-1], store, where, index)
    first += project(1, first)
    early.append(reduce(jnp.concatenate([first, project(2, first)], 0)))
    early = jnp.concatenate(early, 0)
    early = jnp.concatenate([early, swap(early, row_flip=0, feat_flip=1)], 1)
    early = [early] + [cross(early, flip) for flip in range(1, row_groups)]

    middle = project(3, early[0])
    middle_totals = list(totals(halves(middle)))
    middle = whiten(middle_totals[-1])
    late = project(4, middle_totals[1])
    late += project(5, late, middle)
    late += project(6, late)
    late = jnp.concatenate([middle, reduce(late)], 0)
    late = jnp.concatenate([late] + [cross(late, flip) for flip in range(1, row_groups)], 0)
    pair = swap(late, row_flip=0, feat_flip=1)
    return score(where, early, late, pair, store, index, rows, rows - near)


def plain(slab_grads, basis, eigenvalues, store_rows, slab_index, *, row_groups, feat_groups):
    store_count = store_rows.shape[0]
    first_column = (lax.axis_index("rows") * feat_groups + lax.axis_index("feat")) * store_count
    columns = first_column + jnp.arange(store_count, dtype=jnp.int32)
    local_dirs = basis.shape[1]
    partial_value = jnp.dot(
        lax.all_gather(slab_grads, "rows", axis=0, tiled=True),
        basis,
        preferred_element_type=jnp.float32,
    )
    summed = lax.psum(partial_value, "feat")
    scales = lax.dynamic_slice_in_dim(
        eigenvalues, lax.axis_index("rows") * local_dirs, local_dirs, 0
    )
    whitened = (summed / (scales + DAMPING)).astype(jnp.bfloat16)
    gathered = lax.all_gather(whitened, "rows", axis=1, tiled=True)
    product = lax.dot_general(
        gathered, store_rows, CONTRACT_LAST, preferred_element_type=jnp.float32
    )
    return jnp.where(slab_index[:, None] == columns[None, :], jnp.zeros_like(product), product)


def solution(mesh):
    row_groups, feat_groups = mesh.shape["rows"], mesh.shape["feat"]
    powers = all(n > 1 and n & (n - 1) == 0 for n in (row_groups, feat_groups))

    def body(*args):
        sizes = dict(row_groups=row_groups, feat_groups=feat_groups)
        rows = args[0].shape[0]
        if not powers or rows < 96 or rows % 16 or args[1].shape[1] % 2:
            return plain(*args, **sizes)
        return shards(*args, **sizes)

    in_specs = (P("rows", "feat"), P("feat", "rows"), P(), P(("rows", "feat"), None), P())
    out_specs = P(None, ("rows", "feat"))
    return jax.shard_map(body, mesh=mesh, in_specs=in_specs, out_specs=out_specs, check_vma=False)
```

```python
import functools

import jax
import jax.numpy as jnp
from jax import lax
from jax.experimental import pallas as pl
from jax.sharding import PartitionSpec as P


DAMPING = 0.1
CONTRACT_LAST = (((1,), (1,)), ((), ()))


def parity(number, count):
    bits = 0
    while count > 1:
        bits = bits ^ number
        number = number >> 1
        count //= 2
    return bits & 1


def exchange(value, row_groups, feat_groups, row_flip, feat_flip):
    count = row_groups * feat_groups
    pairs = [
        (i, (((i // feat_groups) ^ row_flip) * feat_groups) + ((i % feat_groups) ^ feat_flip))
        for i in range(count)
    ]
    return lax.ppermute(value, ("rows", "feat"), pairs)


def after(value, *needed):
    return lax.optimization_barrier((value, *needed))[0]


def score(row, early, late, pair, store, same, rows, tail):
    row_groups = len(early)
    columns = []
    for flip in range(row_groups):
        spot = flip * tail
        whole = jnp.concatenate(
            [
                early[flip],
                jnp.concatenate([late[spot : spot + tail], pair[spot : spot + tail]], 1),
            ],
            0,
        )
        columns.append([whole[i * rows : (i + 1) * rows] for i in range(row_groups)])
    blocks = [
        jnp.concatenate([columns[flip][place ^ flip] for flip in range(row_groups)], 1)
        for place in range(row_groups)
    ]
    bit = 1
    while bit < row_groups:
        moved = (row & bit) != 0
        blocks = [
            jnp.where(moved, blocks[place ^ bit], blocks[place]) for place in range(row_groups)
        ]
        bit *= 2
    product = lax.dot_general(
        jnp.concatenate(blocks, 0), store, CONTRACT_LAST, preferred_element_type=jnp.float32
    )
    return jnp.where(same(product.shape), jnp.zeros_like(product), product)


def dot_kernel(left_ref, right_ref, out_ref):
    term = jnp.dot(left_ref[...], right_ref[...], preferred_element_type=jnp.float32)

    @pl.when(pl.program_id(0) == 0)
    def _():
        out_ref[...] = term

    @pl.when(pl.program_id(0) > 0)
    def _():
        out_ref[...] += term


def dot(left, right):
    depth = left.shape[1]
    block = depth // 16 if depth % 2048 == 0 else depth
    rows, columns = left.shape[0], right.shape[1]
    return pl.pallas_call(
        dot_kernel,
        out_shape=jax.ShapeDtypeStruct((rows, columns), jnp.float32),
        grid=(depth // block,),
        in_specs=[
            pl.BlockSpec((rows, block), lambda k: (0, k)),
            pl.BlockSpec((block, columns), lambda k: (k, 0)),
        ],
        out_specs=pl.BlockSpec((rows, columns), lambda k: (0, 0)),
        cost_estimate=pl.CostEstimate(
            flops=2 * rows * depth * columns,
            bytes_accessed=2 * depth * (rows + columns) + 4 * rows * columns,
            transcendentals=0,
        ),
        name="dot",
    )(left, right)


def shards(slab_grads, basis, eigenvalues, store_rows, slab_index, *, row_groups, feat_groups):
    row, feat = lax.axis_index("rows"), lax.axis_index("feat")
    store_count = store_rows.shape[0]
    first_column = (row * feat_groups + feat) * store_count
    rows, features = slab_grads.shape
    directions = basis.shape[1]
    half = directions // 2
    side = parity(row, row_groups) ^ parity(feat, feat_groups)
    swap = functools.partial(exchange, row_groups=row_groups, feat_groups=feat_groups)

    def cross(value, flip):
        return swap(value, row_flip=flip, feat_flip=bin(flip).count("1") & 1)

    ends = [rows * 43 // 100, rows * 68 // 100, rows * 90 // 100, rows]
    ends = [end // 8 * 8 for end in ends]
    lead = min(32, ends[0] // 16 * 8)
    unit = features // 8
    plan = [
        (0, lead, (0, 2 * unit, features)),
        (lead, ends[0], (0, features)),
        (ends[0], ends[1], (0, features)),
        (ends[1], ends[2], (0, 6 * unit, features)),
        (ends[2], ends[3], (0, 4 * unit, 7 * unit, features)),
    ]
    cuts = [
        (r0, r1, f0, f1) for r0, r1, marks in plan for f0, f1 in zip(marks[:-1], marks[1:])
    ]

    last = row_groups - 1
    far = [swap(slab_grads, row_flip=flip, feat_flip=0) for flip in range(1, last)]
    pieces, ready = [], slab_grads
    for i, (r0, r1, f0, f1) in enumerate(cuts):
        pieces.append(ready[r0:r1, f0:f1])
        if i < 3:
            ready = after(slab_grads, pieces[-1])
    moved = []
    for piece in pieces:
        moved.append(swap(piece, row_flip=last, feat_flip=0))

    scales = lax.dynamic_slice_in_dim(
        eigenvalues, row * directions + side * half, half, 0
    )[None, :] + DAMPING
    order = []
    for flip in range(row_groups):
        base = (row ^ flip) * directions
        for part in (side, 1 - side):
            order.append(lax.dynamic_slice_in_dim(store_rows, base + part * half, half, 1))
    store = jnp.concatenate(order, 1)

    def same(shape):
        return slab_index[:, None] == first_column + lax.broadcasted_iota(jnp.int32, shape, 1)

    def project(i, *needed):
        _, _, f0, f1 = cuts[i]
        return jnp.dot(
            after(moved[i], *needed), basis[f0:f1], preferred_element_type=jnp.float32
        )

    def halves(partial_value):
        mine = lax.dynamic_slice_in_dim(partial_value, side * half, half, 1)
        other = lax.dynamic_slice_in_dim(partial_value, (1 - side) * half, half, 1)
        return mine + swap(other, row_flip=0, feat_flip=1)

    def totals(total):
        yield total
        bit = 2
        while bit < feat_groups:
            total = total + swap(total, row_flip=0, feat_flip=bit | 1)
            bit *= 2
            yield total

    def whiten(total):
        return (total / scales).astype(jnp.bfloat16)

    def reduce(partial_value):
        return whiten(list(totals(halves(partial_value)))[-1])

    blocks = [after(slab_grads, *pieces)] + far
    early = []
    for block in blocks:
        value = dot(after(block, *early), basis)
        early.append(reduce(value))
    first = project(0, early[-1], store)
    first += project(1, first)
    early.append(reduce(jnp.concatenate([first, project(2, first)], 0)))
    early.append(reduce(project(3, early[-1])))
    early = jnp.concatenate(early, 0)
    early = jnp.concatenate([early, swap(early, row_flip=0, feat_flip=1)], 1)
    early = [early] + [cross(early, flip) for flip in range(1, row_groups)]

    middle = project(4, early[0])
    middle += project(5, middle)
    middle_totals = list(totals(halves(middle)))
    middle = whiten(middle_totals[-1])
    late = project(6, middle_totals[1])
    late += project(7, late, middle_totals[2])
    late += project(8, late, middle)
    late = jnp.concatenate([middle, reduce(late)], 0)
    late = jnp.concatenate([late] + [cross(late, flip) for flip in range(1, row_groups)], 0)
    pair = swap(late, row_flip=0, feat_flip=1)
    return score(row, early, late, pair, store, same, rows, rows - ends[1])


def plain(slab_grads, basis, eigenvalues, store_rows, slab_index, *, row_groups, feat_groups):
    store_count = store_rows.shape[0]
    first_column = (lax.axis_index("rows") * feat_groups + lax.axis_index("feat")) * store_count
    columns = first_column + jnp.arange(store_count, dtype=jnp.int32)
    local_dirs = basis.shape[1]
    partial_value = jnp.dot(
        lax.all_gather(slab_grads, "rows", axis=0, tiled=True),
        basis,
        preferred_element_type=jnp.float32,
    )
    summed = lax.psum(partial_value, "feat")
    scales = lax.dynamic_slice_in_dim(
        eigenvalues, lax.axis_index("rows") * local_dirs, local_dirs, 0
    )
    whitened = (summed / (scales + DAMPING)).astype(jnp.bfloat16)
    gathered = lax.all_gather(whitened, "rows", axis=1, tiled=True)
    product = lax.dot_general(
        gathered, store_rows, CONTRACT_LAST, preferred_element_type=jnp.float32
    )
    return jnp.where(slab_index[:, None] == columns[None, :], jnp.zeros_like(product), product)


def solution(mesh):
    row_groups, feat_groups = mesh.shape["rows"], mesh.shape["feat"]
    powers = all(n > 1 and n & (n - 1) == 0 for n in (row_groups, feat_groups))

    def body(*args):
        sizes = dict(row_groups=row_groups, feat_groups=feat_groups)
        rows = args[0].shape[0]
        if not powers or rows < 96 or rows % 16 or args[1].shape[1] % 2:
            return plain(*args, **sizes)
        return shards(*args, **sizes)

    in_specs = (P("rows", "feat"), P("feat", "rows"), P(), P(("rows", "feat"), None), P())
    out_specs = P(None, ("rows", "feat"))
    return jax.shard_map(body, mesh=mesh, in_specs=in_specs, out_specs=out_specs, check_vma=False)
```

```python
import functools

import jax
import jax.numpy as jnp
from jax import lax
from jax.experimental import pallas as pl
from jax.experimental.pallas import tpu as pltpu
from jax.sharding import PartitionSpec as P


DAMPING = 0.1
CONTRACT_LAST = (((1,), (1,)), ((), ()))


def parity(number, count):
    bits = 0
    while count > 1:
        bits = bits ^ number
        number = number >> 1
        count //= 2
    return bits & 1


def exchange(value, row_groups, feat_groups, row_flip, feat_flip):
    count = row_groups * feat_groups
    pairs = [
        (i, (((i // feat_groups) ^ row_flip) * feat_groups) + ((i % feat_groups) ^ feat_flip))
        for i in range(count)
    ]
    return lax.ppermute(value, ("rows", "feat"), pairs)


def after(value, *needed):
    return lax.optimization_barrier((value, *needed))[0]


def score(row, early, late, pair, store, same, rows, tail):
    row_groups = len(early)
    columns = []
    for flip in range(row_groups):
        spot = flip * tail
        whole = jnp.concatenate(
            [
                early[flip],
                jnp.concatenate([late[spot : spot + tail], pair[spot : spot + tail]], 1),
            ],
            0,
        )
        columns.append([whole[i * rows : (i + 1) * rows] for i in range(row_groups)])
    blocks = [
        jnp.concatenate([columns[flip][place ^ flip] for flip in range(row_groups)], 1)
        for place in range(row_groups)
    ]
    bit = 1
    while bit < row_groups:
        moved = (row & bit) != 0
        blocks = [
            jnp.where(moved, blocks[place ^ bit], blocks[place]) for place in range(row_groups)
        ]
        bit *= 2
    product = lax.dot_general(
        jnp.concatenate(blocks, 0), store, CONTRACT_LAST, preferred_element_type=jnp.float32
    )
    return jnp.where(same(product.shape), jnp.zeros_like(product), product)


def dot_kernel(left_ref, right_ref, out_ref):
    term = jnp.dot(left_ref[...], right_ref[...], preferred_element_type=jnp.float32)

    @pl.when(pl.program_id(0) == 0)
    def _():
        out_ref[...] = term

    @pl.when(pl.program_id(0) > 0)
    def _():
        out_ref[...] += term


def head_kernel(rows, columns, whole_ref, out_ref, arrived):
    copy = pltpu.make_async_copy(
        whole_ref.at[pl.ds(0, rows), pl.ds(0, columns)], out_ref, arrived
    )
    copy.start()
    copy.wait()


def head(whole, rows, columns):
    return pl.pallas_call(
        functools.partial(head_kernel, rows, columns),
        out_shape=pltpu.VMEM((rows, columns), whole.dtype),
        in_specs=[pl.BlockSpec(memory_space=pl.ANY)],
        out_specs=pl.BlockSpec(memory_space=pltpu.VMEM),
        scratch_shapes=[pltpu.SemaphoreType.DMA],
        name="head",
    )(whole)


def dot(left, right):
    depth = left.shape[1]
    block = depth // 16 if depth % 2048 == 0 else depth
    rows, columns = left.shape[0], right.shape[1]
    return pl.pallas_call(
        dot_kernel,
        out_shape=jax.ShapeDtypeStruct((rows, columns), jnp.float32),
        grid=(depth // block,),
        in_specs=[
            pl.BlockSpec((rows, block), lambda k: (0, k)),
            pl.BlockSpec((block, columns), lambda k: (k, 0)),
        ],
        out_specs=pl.BlockSpec((rows, columns), lambda k: (0, 0)),
        cost_estimate=pl.CostEstimate(
            flops=2 * rows * depth * columns,
            bytes_accessed=2 * depth * (rows + columns) + 4 * rows * columns,
            transcendentals=0,
        ),
        name="dot",
    )(left, right)


def shards(slab_grads, basis, eigenvalues, store_rows, slab_index, *, row_groups, feat_groups):
    row, feat = lax.axis_index("rows"), lax.axis_index("feat")
    store_count = store_rows.shape[0]
    first_column = (row * feat_groups + feat) * store_count
    rows, features = slab_grads.shape
    directions = basis.shape[1]
    half = directions // 2
    side = parity(row, row_groups) ^ parity(feat, feat_groups)
    swap = functools.partial(exchange, row_groups=row_groups, feat_groups=feat_groups)

    def cross(value, flip):
        return swap(value, row_flip=flip, feat_flip=bin(flip).count("1") & 1)

    ends = [rows * 43 // 100, rows * 68 // 100, rows * 90 // 100, rows]
    ends = [end // 8 * 8 for end in ends]
    lead = min(32, ends[0] // 16 * 8)
    unit = features // 8
    plan = [
        (0, lead, (0, 2 * unit, features)),
        (lead, ends[0], (0, features)),
        (ends[0], ends[1], (0, features)),
        (ends[1], ends[2], (0, 6 * unit, features)),
        (ends[2], ends[3], (0, 4 * unit, 7 * unit, features)),
    ]
    cuts = [
        (r0, r1, f0, f1) for r0, r1, marks in plan for f0, f1 in zip(marks[:-1], marks[1:])
    ]

    last = row_groups - 1
    far = [swap(slab_grads, row_flip=flip, feat_flip=0) for flip in range(1, last)]
    pieces, ready = [], slab_grads
    for i, (r0, r1, f0, f1) in enumerate(cuts):
        pieces.append(head(ready, r1, f1) if i == 0 else ready[r0:r1, f0:f1])
        if i < 3:
            ready = after(slab_grads, pieces[-1])
    moved = []
    for piece in pieces:
        moved.append(swap(piece, row_flip=last, feat_flip=0))

    scales = lax.dynamic_slice_in_dim(
        eigenvalues, row * directions + side * half, half, 0
    )[None, :] + DAMPING
    order = []
    for flip in range(row_groups):
        base = (row ^ flip) * directions
        for part in (side, 1 - side):
            order.append(lax.dynamic_slice_in_dim(store_rows, base + part * half, half, 1))
    store = jnp.concatenate(order, 1)

    def same(shape):
        return slab_index[:, None] == first_column + lax.broadcasted_iota(jnp.int32, shape, 1)

    def project(i, *needed):
        _, _, f0, f1 = cuts[i]
        return jnp.dot(
            after(moved[i], *needed), basis[f0:f1], preferred_element_type=jnp.float32
        )

    def halves(partial_value):
        mine = lax.dynamic_slice_in_dim(partial_value, side * half, half, 1)
        other = lax.dynamic_slice_in_dim(partial_value, (1 - side) * half, half, 1)
        return mine + swap(other, row_flip=0, feat_flip=1)

    def totals(total):
        yield total
        bit = 2
        while bit < feat_groups:
            total = total + swap(total, row_flip=0, feat_flip=bit | 1)
            bit *= 2
            yield total

    def whiten(total):
        return (total / scales).astype(jnp.bfloat16)

    def reduce(partial_value):
        return whiten(list(totals(halves(partial_value)))[-1])

    blocks = [after(slab_grads, moved[0], *pieces)] + far
    early = []
    for block in blocks:
        value = dot(after(block, *early), basis)
        early.append(reduce(value))
    first = project(0, early[-1], store)
    first += project(1, first)
    early.append(reduce(jnp.concatenate([first, project(2, first)], 0)))
    early.append(reduce(project(3, early[-1])))
    early = jnp.concatenate(early, 0)
    early = jnp.concatenate([early, swap(early, row_flip=0, feat_flip=1)], 1)
    early = [early] + [cross(early, flip) for flip in range(1, row_groups)]

    middle = project(4, early[0])
    middle += project(5, middle)
    middle_totals = list(totals(halves(middle)))
    middle = whiten(middle_totals[-1])
    late = project(6, middle_totals[1])
    late += project(7, late, middle_totals[2])
    late += project(8, late, middle)
    late = jnp.concatenate([middle, reduce(late)], 0)
    late = jnp.concatenate([late] + [cross(late, flip) for flip in range(1, row_groups)], 0)
    pair = swap(late, row_flip=0, feat_flip=1)
    return score(row, early, late, pair, store, same, rows, rows - ends[1])


def plain(slab_grads, basis, eigenvalues, store_rows, slab_index, *, row_groups, feat_groups):
    store_count = store_rows.shape[0]
    first_column = (lax.axis_index("rows") * feat_groups + lax.axis_index("feat")) * store_count
    columns = first_column + jnp.arange(store_count, dtype=jnp.int32)
    local_dirs = basis.shape[1]
    partial_value = jnp.dot(
        lax.all_gather(slab_grads, "rows", axis=0, tiled=True),
        basis,
        preferred_element_type=jnp.float32,
    )
    summed = lax.psum(partial_value, "feat")
    scales = lax.dynamic_slice_in_dim(
        eigenvalues, lax.axis_index("rows") * local_dirs, local_dirs, 0
    )
    whitened = (summed / (scales + DAMPING)).astype(jnp.bfloat16)
    gathered = lax.all_gather(whitened, "rows", axis=1, tiled=True)
    product = lax.dot_general(
        gathered, store_rows, CONTRACT_LAST, preferred_element_type=jnp.float32
    )
    return jnp.where(slab_index[:, None] == columns[None, :], jnp.zeros_like(product), product)


def solution(mesh):
    row_groups, feat_groups = mesh.shape["rows"], mesh.shape["feat"]
    powers = all(n > 1 and n & (n - 1) == 0 for n in (row_groups, feat_groups))

    def body(*args):
        sizes = dict(row_groups=row_groups, feat_groups=feat_groups)
        rows = args[0].shape[0]
        if not powers or rows < 96 or rows % 16 or args[1].shape[1] % 2:
            return plain(*args, **sizes)
        return shards(*args, **sizes)

    in_specs = (P("rows", "feat"), P("feat", "rows"), P(), P(("rows", "feat"), None), P())
    out_specs = P(None, ("rows", "feat"))
    return jax.shard_map(body, mesh=mesh, in_specs=in_specs, out_specs=out_specs, check_vma=False)
```

```python
import functools

import jax
import jax.numpy as jnp
from jax import lax
from jax.experimental import pallas as pl
from jax.experimental.pallas import tpu as pltpu
from jax.sharding import PartitionSpec as P


DAMPING = 0.1
CONTRACT_LAST = (((1,), (1,)), ((), ()))


def parity(number, count):
    bits = 0
    while count > 1:
        bits = bits ^ number
        number = number >> 1
        count //= 2
    return bits & 1


def exchange(value, row_groups, feat_groups, row_flip, feat_flip):
    count = row_groups * feat_groups
    pairs = [
        (i, (((i // feat_groups) ^ row_flip) * feat_groups) + ((i % feat_groups) ^ feat_flip))
        for i in range(count)
    ]
    return lax.ppermute(value, ("rows", "feat"), pairs)


def after(value, *needed):
    return lax.optimization_barrier((value, *needed))[0]


def place(row, blocks):
    row_groups, bit = len(blocks), 1
    while bit < row_groups:
        moved = (row & bit) != 0
        blocks = [jnp.where(moved, blocks[a ^ bit], blocks[a]) for a in range(row_groups)]
        bit *= 2
    return jnp.concatenate(blocks, 0)


def product(left, right):
    return lax.dot_general(left, right, CONTRACT_LAST, preferred_element_type=jnp.float32)


def arrange(row, early, rows, tail):
    row_groups, width = len(early), early[0].shape[1]
    blocks = []
    for a in range(row_groups):
        parts = []
        for flip in range(row_groups):
            spot = (a ^ flip) * rows
            if a ^ flip == row_groups - 1:
                part = early[flip][spot : spot + rows - tail]
                part = jnp.concatenate([part, jnp.zeros((tail, width), part.dtype)], 0)
            else:
                part = early[flip][spot : spot + rows]
            parts.append(part)
        blocks.append(jnp.concatenate(parts, 1))
    return place(row, blocks)


def partial_scores(early, store, rows, tail):
    row_groups, width = len(early), early[0].shape[1]
    values = []
    for a in range(row_groups):
        total = 0.0
        for flip in range(row_groups):
            end = ((a ^ flip) + 1) * rows
            if a ^ flip != row_groups - 1:
                total += product(
                    early[flip][end - tail : end], store[:, flip * width : (flip + 1) * width]
                )
        values.append(total)
    return jnp.concatenate(values, 0)


def masked_product(whitened, store, slab_index):
    value = product(whitened, store)
    columns = lax.broadcasted_iota(jnp.int32, value.shape, 1)
    return jnp.where(slab_index[:, None] == columns, jnp.zeros_like(value), value)


def score_late_kernel(
    row_groups, rows, row_ref, late_ref, pair_ref, store_ref, partial_ref, index_ref, _, out_ref,
    held, sent
):
    tail, half = late_ref.shape[0] // row_groups, late_ref.shape[1]
    copies = []
    for a in range(row_groups):
        flip = (row_groups - 1) ^ a
        spot, column = flip * tail, 2 * flip * half
        value = partial_ref[a * tail : (a + 1) * tail, :]
        value += product(
            late_ref[spot : spot + tail, :], store_ref[:, column : column + half]
        )
        value += product(
            pair_ref[spot : spot + tail, :], store_ref[:, column + half : column + 2 * half]
        )
        block = row_ref[0] ^ a
        index = index_ref[pl.ds(pl.multiple_of(block * tail, 8), tail), :]
        columns = lax.broadcasted_iota(jnp.int32, value.shape, 1)
        held[a * tail : (a + 1) * tail, :] = jnp.where(
            index == columns, jnp.zeros_like(value), value
        )
        copy = pltpu.make_async_copy(
            held.at[pl.ds(a * tail, tail)],
            out_ref.at[pl.ds(pl.multiple_of(block * rows + rows - tail, 8), tail)],
            sent.at[a],
        )
        copy.start()
        copies.append(copy)
    for copy in copies:
        copy.wait()


def score_late(row, late, pair, store, partial_value, index, value, row_groups):
    rows = value.shape[0] // row_groups
    vmem = pl.BlockSpec(memory_space=pltpu.VMEM)
    return pl.pallas_call(
        functools.partial(score_late_kernel, row_groups, rows),
        out_shape=jax.ShapeDtypeStruct(value.shape, value.dtype),
        in_specs=[pl.BlockSpec(memory_space=pltpu.SMEM)]
        + [vmem] * 5
        + [pl.BlockSpec(memory_space=pl.ANY)],
        out_specs=pl.BlockSpec(memory_space=pl.ANY),
        scratch_shapes=[
            pltpu.VMEM(partial_value.shape, jnp.float32),
            pltpu.SemaphoreType.DMA((row_groups,)),
        ],
        input_output_aliases={6: 0},
        compiler_params=pltpu.CompilerParams(vmem_limit_bytes=16 << 20),
        name="score_late",
    )(row.astype(jnp.int32).reshape(1), late, pair, store, partial_value, index, value)


def dot_kernel(left_ref, right_ref, out_ref):
    term = jnp.dot(left_ref[...], right_ref[...], preferred_element_type=jnp.float32)

    @pl.when(pl.program_id(0) == 0)
    def _():
        out_ref[...] = term

    @pl.when(pl.program_id(0) > 0)
    def _():
        out_ref[...] += term


def head_kernel(rows, columns, whole_ref, out_ref, arrived):
    copy = pltpu.make_async_copy(
        whole_ref.at[pl.ds(0, rows), pl.ds(0, columns)], out_ref, arrived
    )
    copy.start()
    copy.wait()


def head(whole, rows, columns):
    return pl.pallas_call(
        functools.partial(head_kernel, rows, columns),
        out_shape=pltpu.VMEM((rows, columns), whole.dtype),
        in_specs=[pl.BlockSpec(memory_space=pl.ANY)],
        out_specs=pl.BlockSpec(memory_space=pltpu.VMEM),
        scratch_shapes=[pltpu.SemaphoreType.DMA],
        name="head",
    )(whole)


def dot(left, right):
    depth = left.shape[1]
    block = depth // 16 if depth % 2048 == 0 else depth
    rows, columns = left.shape[0], right.shape[1]
    return pl.pallas_call(
        dot_kernel,
        out_shape=jax.ShapeDtypeStruct((rows, columns), jnp.float32),
        grid=(depth // block,),
        in_specs=[
            pl.BlockSpec((rows, block), lambda k: (0, k)),
            pl.BlockSpec((block, columns), lambda k: (k, 0)),
        ],
        out_specs=pl.BlockSpec((rows, columns), lambda k: (0, 0)),
        cost_estimate=pl.CostEstimate(
            flops=2 * rows * depth * columns,
            bytes_accessed=2 * depth * (rows + columns) + 4 * rows * columns,
            transcendentals=0,
        ),
        name="dot",
    )(left, right)


def shards(slab_grads, basis, eigenvalues, store_rows, slab_index, *, row_groups, feat_groups):
    row, feat = lax.axis_index("rows"), lax.axis_index("feat")
    store_count = store_rows.shape[0]
    first_column = (row * feat_groups + feat) * store_count
    rows, features = slab_grads.shape
    directions = basis.shape[1]
    half = directions // 2
    side = parity(row, row_groups) ^ parity(feat, feat_groups)
    swap = functools.partial(exchange, row_groups=row_groups, feat_groups=feat_groups)

    def cross(value, flip):
        return swap(value, row_flip=flip, feat_flip=bin(flip).count("1") & 1)

    ends = [rows * 43 // 100, rows * 68 // 100, rows * 90 // 100, rows]
    ends = [end // 8 * 8 for end in ends]
    lead = min(32, ends[0] // 16 * 8)
    unit = features // 8
    plan = [
        (0, lead, (0, 2 * unit, features)),
        (lead, ends[0], (0, features)),
        (ends[0], ends[1], (0, features)),
        (ends[1], ends[2], (0, 6 * unit, features)),
        (ends[2], ends[3], (0, 4 * unit, 7 * unit, features)),
    ]
    cuts = [
        (r0, r1, f0, f1) for r0, r1, marks in plan for f0, f1 in zip(marks[:-1], marks[1:])
    ]

    last = row_groups - 1
    far = [swap(slab_grads, row_flip=flip, feat_flip=0) for flip in range(1, last)]
    pieces, ready = [], slab_grads
    for i, (r0, r1, f0, f1) in enumerate(cuts):
        pieces.append(head(ready, r1, f1) if i == 0 else ready[r0:r1, f0:f1])
        if i < 3:
            ready = after(slab_grads, pieces[-1])
    moved = []
    for piece in pieces:
        moved.append(swap(piece, row_flip=last, feat_flip=0))

    scales = lax.dynamic_slice_in_dim(
        eigenvalues, row * directions + side * half, half, 0
    )[None, :] + DAMPING
    order = []
    for flip in range(row_groups):
        base = (row ^ flip) * directions
        for part in (side, 1 - side):
            order.append(lax.dynamic_slice_in_dim(store_rows, base + part * half, half, 1))
    store = jnp.concatenate(order, 1)

    tail = rows - ends[1]
    shifted = slab_index - first_column
    index = shifted.reshape(row_groups, rows)[:, rows - tail :].reshape(row_groups * tail, 1)

    def project(i, *needed):
        _, _, f0, f1 = cuts[i]
        return jnp.dot(
            after(moved[i], *needed), basis[f0:f1], preferred_element_type=jnp.float32
        )

    def halves(partial_value):
        mine = lax.dynamic_slice_in_dim(partial_value, side * half, half, 1)
        other = lax.dynamic_slice_in_dim(partial_value, (1 - side) * half, half, 1)
        return mine + swap(other, row_flip=0, feat_flip=1)

    def totals(total):
        yield total
        bit = 2
        while bit < feat_groups:
            total = total + swap(total, row_flip=0, feat_flip=bit | 1)
            bit *= 2
            yield total

    def whiten(total):
        return (total / scales).astype(jnp.bfloat16)

    def reduce(partial_value):
        return whiten(list(totals(halves(partial_value)))[-1])

    blocks = [after(slab_grads, moved[0], *pieces)] + far
    early = []
    for block in blocks:
        value = dot(after(block, *early), basis)
        early.append(reduce(value))
    first = project(0, early[-1])
    first += project(1, first)
    early.append(reduce(jnp.concatenate([first, project(2, first)], 0)))
    early.append(reduce(project(3, early[-1])))
    early = jnp.concatenate(early, 0)
    early = jnp.concatenate([early, swap(early, row_flip=0, feat_flip=1)], 1)
    early = [early] + [cross(early, flip) for flip in range(1, row_groups)]

    middle = project(4, early[0])
    middle += project(5, middle)
    middle_totals = list(totals(halves(middle)))
    middle = whiten(middle_totals[-1])
    late = project(6, middle_totals[1])
    late += project(7, late, middle_totals[2])
    late += project(8, late, middle)
    late_totals = list(totals(halves(late)))
    late = whiten(after(late_totals[-1], *early[1:]))
    others = [after(part, late) for part in early[1:]]
    whitened = arrange(row, [early[0]] + others, rows, tail)
    value = masked_product(whitened, store, shifted)
    others = [after(part, value) for part in early]
    partial_value = partial_scores(others, store, rows, tail)
    late = jnp.concatenate([middle, late], 0)
    others = [cross(late, flip) for flip in range(1, row_groups)]
    late = jnp.concatenate([late] + others, 0)
    pair = swap(after(late, value), row_flip=0, feat_flip=1)
    return score_late(row, late, pair, store, partial_value, index, value, row_groups)


def plain(slab_grads, basis, eigenvalues, store_rows, slab_index, *, row_groups, feat_groups):
    store_count = store_rows.shape[0]
    first_column = (lax.axis_index("rows") * feat_groups + lax.axis_index("feat")) * store_count
    columns = first_column + jnp.arange(store_count, dtype=jnp.int32)
    local_dirs = basis.shape[1]
    partial_value = jnp.dot(
        lax.all_gather(slab_grads, "rows", axis=0, tiled=True),
        basis,
        preferred_element_type=jnp.float32,
    )
    summed = lax.psum(partial_value, "feat")
    scales = lax.dynamic_slice_in_dim(
        eigenvalues, lax.axis_index("rows") * local_dirs, local_dirs, 0
    )
    whitened = (summed / (scales + DAMPING)).astype(jnp.bfloat16)
    gathered = lax.all_gather(whitened, "rows", axis=1, tiled=True)
    product = lax.dot_general(
        gathered, store_rows, CONTRACT_LAST, preferred_element_type=jnp.float32
    )
    return jnp.where(slab_index[:, None] == columns[None, :], jnp.zeros_like(product), product)


def solution(mesh):
    row_groups, feat_groups = mesh.shape["rows"], mesh.shape["feat"]
    powers = all(n > 1 and n & (n - 1) == 0 for n in (row_groups, feat_groups))

    def body(*args):
        sizes = dict(row_groups=row_groups, feat_groups=feat_groups)
        rows = args[0].shape[0]
        if not powers or rows < 96 or rows % 16 or args[1].shape[1] % 2:
            return plain(*args, **sizes)
        return shards(*args, **sizes)

    in_specs = (P("rows", "feat"), P("feat", "rows"), P(), P(("rows", "feat"), None), P())
    out_specs = P(None, ("rows", "feat"))
    return jax.shard_map(body, mesh=mesh, in_specs=in_specs, out_specs=out_specs, check_vma=False)
```

```python
import functools

import jax
import jax.numpy as jnp
from jax import lax
from jax.experimental import pallas as pl
from jax.experimental.pallas import tpu as pltpu
from jax.sharding import PartitionSpec as P


DAMPING = 0.1
CONTRACT_LAST = (((1,), (1,)), ((), ()))


def parity(number, count):
    bits = 0
    while count > 1:
        bits = bits ^ number
        number = number >> 1
        count //= 2
    return bits & 1


def exchange(value, row_groups, feat_groups, row_flip, feat_flip):
    count = row_groups * feat_groups
    pairs = [
        (i, (((i // feat_groups) ^ row_flip) * feat_groups) + ((i % feat_groups) ^ feat_flip))
        for i in range(count)
    ]
    return lax.ppermute(value, ("rows", "feat"), pairs)


def after(value, *needed):
    return lax.optimization_barrier((value, *needed))[0]


def place(row, blocks):
    row_groups, bit = len(blocks), 1
    while bit < row_groups:
        moved = (row & bit) != 0
        blocks = [jnp.where(moved, blocks[a ^ bit], blocks[a]) for a in range(row_groups)]
        bit *= 2
    return jnp.concatenate(blocks, 0)


def product(left, right):
    return lax.dot_general(left, right, CONTRACT_LAST, preferred_element_type=jnp.float32)


def arrange(row, early, rows, tail):
    row_groups, width = len(early), early[0].shape[1]
    blocks = []
    for a in range(row_groups):
        parts = []
        for flip in range(row_groups):
            spot = (a ^ flip) * rows
            if a ^ flip == row_groups - 1:
                part = early[flip][spot : spot + rows - tail]
                part = jnp.concatenate([part, jnp.zeros((tail, width), part.dtype)], 0)
            else:
                part = early[flip][spot : spot + rows]
            parts.append(part)
        blocks.append(jnp.concatenate(parts, 1))
    return place(row, blocks)


def partial_scores(early, late, store, rows, tail):
    row_groups, width = len(early), early[0].shape[1]
    half = width // 2
    values = []
    for a in range(row_groups):
        left, right = [], []
        for flip in range(row_groups):
            end = ((a ^ flip) + 1) * rows
            if a ^ flip != row_groups - 1:
                left.append(early[flip][end - tail : end])
                right.append(store[:, flip * width : (flip + 1) * width])
            else:
                left.append(late[flip * tail : (flip + 1) * tail])
                right.append(store[:, flip * width : flip * width + half])
        total = product(jnp.concatenate(left, 1), jnp.concatenate(right, 1))
        values.append(total)
    return jnp.concatenate(values, 0)


def masked_product(whitened, store, slab_index):
    value = product(whitened, store)
    columns = lax.broadcasted_iota(jnp.int32, value.shape, 1)
    return jnp.where(slab_index[:, None] == columns, jnp.zeros_like(value), value)


def score_late_kernel(
    row_groups, rows, row_ref, pair_ref, store_ref, partial_ref, index_ref, _, out_ref, held, sent
):
    tail, half = pair_ref.shape[0] // row_groups, pair_ref.shape[1]
    copies = []
    for a in range(row_groups):
        flip = (row_groups - 1) ^ a
        spot = flip * tail
        value = partial_ref[a * tail : (a + 1) * tail, :]
        value += product(
            pair_ref[spot : spot + tail, :], store_ref[:, flip * half : (flip + 1) * half]
        )
        block = row_ref[0] ^ a
        index = index_ref[pl.ds(pl.multiple_of(block * tail, 8), tail), :]
        columns = lax.broadcasted_iota(jnp.int32, value.shape, 1)
        held[a * tail : (a + 1) * tail, :] = jnp.where(
            index == columns, jnp.zeros_like(value), value
        )
        copy = pltpu.make_async_copy(
            held.at[pl.ds(a * tail, tail)],
            out_ref.at[pl.ds(pl.multiple_of(block * rows + rows - tail, 8), tail)],
            sent.at[a],
        )
        copy.start()
        copies.append(copy)
    for copy in copies:
        copy.wait()


def score_late(row, pair, store, partial_value, index, value, row_groups):
    rows = value.shape[0] // row_groups
    vmem = pl.BlockSpec(memory_space=pltpu.VMEM)
    return pl.pallas_call(
        functools.partial(score_late_kernel, row_groups, rows),
        out_shape=jax.ShapeDtypeStruct(value.shape, value.dtype),
        in_specs=[pl.BlockSpec(memory_space=pltpu.SMEM)]
        + [vmem] * 4
        + [pl.BlockSpec(memory_space=pl.ANY)],
        out_specs=pl.BlockSpec(memory_space=pl.ANY),
        scratch_shapes=[
            pltpu.VMEM(partial_value.shape, jnp.float32),
            pltpu.SemaphoreType.DMA((row_groups,)),
        ],
        input_output_aliases={5: 0},
        compiler_params=pltpu.CompilerParams(vmem_limit_bytes=16 << 20),
        name="score_late",
    )(row.astype(jnp.int32).reshape(1), pair, store, partial_value, index, value)


def dot_kernel(left_ref, right_ref, out_ref):
    term = jnp.dot(left_ref[...], right_ref[...], preferred_element_type=jnp.float32)

    @pl.when(pl.program_id(0) == 0)
    def _():
        out_ref[...] = term

    @pl.when(pl.program_id(0) > 0)
    def _():
        out_ref[...] += term


def head_kernel(rows, columns, whole_ref, out_ref, arrived):
    copy = pltpu.make_async_copy(
        whole_ref.at[pl.ds(0, rows), pl.ds(0, columns)], out_ref, arrived
    )
    copy.start()
    copy.wait()


def head(whole, rows, columns):
    return pl.pallas_call(
        functools.partial(head_kernel, rows, columns),
        out_shape=pltpu.VMEM((rows, columns), whole.dtype),
        in_specs=[pl.BlockSpec(memory_space=pl.ANY)],
        out_specs=pl.BlockSpec(memory_space=pltpu.VMEM),
        scratch_shapes=[pltpu.SemaphoreType.DMA],
        name="head",
    )(whole)


def dot(left, right):
    depth = left.shape[1]
    block = depth // 16 if depth % 2048 == 0 else depth
    rows, columns = left.shape[0], right.shape[1]
    return pl.pallas_call(
        dot_kernel,
        out_shape=jax.ShapeDtypeStruct((rows, columns), jnp.float32),
        grid=(depth // block,),
        in_specs=[
            pl.BlockSpec((rows, block), lambda k: (0, k)),
            pl.BlockSpec((block, columns), lambda k: (k, 0)),
        ],
        out_specs=pl.BlockSpec((rows, columns), lambda k: (0, 0)),
        cost_estimate=pl.CostEstimate(
            flops=2 * rows * depth * columns,
            bytes_accessed=2 * depth * (rows + columns) + 4 * rows * columns,
            transcendentals=0,
        ),
        name="dot",
    )(left, right)


def shards(slab_grads, basis, eigenvalues, store_rows, slab_index, *, row_groups, feat_groups):
    row, feat = lax.axis_index("rows"), lax.axis_index("feat")
    store_count = store_rows.shape[0]
    first_column = (row * feat_groups + feat) * store_count
    rows, features = slab_grads.shape
    directions = basis.shape[1]
    half = directions // 2
    side = parity(row, row_groups) ^ parity(feat, feat_groups)
    swap = functools.partial(exchange, row_groups=row_groups, feat_groups=feat_groups)

    def cross(value, flip):
        return swap(value, row_flip=flip, feat_flip=bin(flip).count("1") & 1)

    ends = [rows * 43 // 100, rows * 68 // 100, rows * 90 // 100, rows]
    ends = [end // 8 * 8 for end in ends]
    lead = min(32, ends[0] // 16 * 8)
    unit = features // 8
    plan = [
        (0, lead, (0, 2 * unit, features)),
        (lead, ends[0], (0, features)),
        (ends[0], ends[1], (0, features)),
        (ends[1], ends[2], (0, 7 * unit, features)),
        (ends[2], ends[3], (0, 4 * unit, 7 * unit + unit // 2, features)),
    ]
    cuts = [
        (r0, r1, f0, f1) for r0, r1, marks in plan for f0, f1 in zip(marks[:-1], marks[1:])
    ]

    last = row_groups - 1
    far = [swap(slab_grads, row_flip=flip, feat_flip=0) for flip in range(1, last)]
    pieces, ready = [], slab_grads
    for i, (r0, r1, f0, f1) in enumerate(cuts):
        pieces.append(head(ready, r1, f1) if i == 0 else ready[r0:r1, f0:f1])
        if i < 3:
            ready = after(slab_grads, pieces[-1])
    moved = []
    for piece in pieces:
        moved.append(swap(piece, row_flip=last, feat_flip=0))

    scales = lax.dynamic_slice_in_dim(
        eigenvalues, row * directions + side * half, half, 0
    )[None, :] + DAMPING
    order = []
    for flip in range(row_groups):
        base = (row ^ flip) * directions
        for part in (side, 1 - side):
            order.append(lax.dynamic_slice_in_dim(store_rows, base + part * half, half, 1))
    store = jnp.concatenate(order, 1)

    tail = rows - ends[1]
    shifted = slab_index - first_column
    index = shifted.reshape(row_groups, rows)[:, rows - tail :].reshape(row_groups * tail, 1)

    def project(i, *needed):
        _, _, f0, f1 = cuts[i]
        return jnp.dot(
            after(moved[i], *needed), basis[f0:f1], preferred_element_type=jnp.float32
        )

    def halves(partial_value):
        mine = lax.dynamic_slice_in_dim(partial_value, side * half, half, 1)
        other = lax.dynamic_slice_in_dim(partial_value, (1 - side) * half, half, 1)
        return mine + swap(other, row_flip=0, feat_flip=1)

    def totals(total):
        yield total
        bit = 2
        while bit < feat_groups:
            total = total + swap(total, row_flip=0, feat_flip=bit | 1)
            bit *= 2
            yield total

    def whiten(total):
        return (total / scales).astype(jnp.bfloat16)

    def reduce(partial_value):
        return whiten(list(totals(halves(partial_value)))[-1])

    blocks = [after(slab_grads, moved[0], *pieces)] + far
    early = []
    for block in blocks:
        value = dot(after(block, *early), basis)
        early.append(reduce(value))
    first = project(0, early[-1])
    first += project(1, first)
    early.append(reduce(jnp.concatenate([first, project(2, first)], 0)))
    early.append(reduce(project(3, early[-1])))
    early = jnp.concatenate(early, 0)
    early = jnp.concatenate([early, swap(early, row_flip=0, feat_flip=1)], 1)
    early = [early] + [cross(early, flip) for flip in range(1, row_groups)]

    middle = project(4, early[0])
    middle += project(5, middle)
    middle_totals = list(totals(halves(middle)))
    middle = whiten(middle_totals[-1])
    late = project(6, middle_totals[1])
    late += project(7, late, middle_totals[2])
    late += project(8, late, middle)
    late_totals = list(totals(halves(late)))
    late = whiten(after(late_totals[-1], *early[1:]))
    others = [after(part, late) for part in early[1:]]
    whitened = arrange(row, [early[0]] + others, rows, tail)
    value = masked_product(whitened, store, shifted)
    late = jnp.concatenate([middle, late], 0)
    others = [cross(late, flip) for flip in range(1, row_groups)]
    late = jnp.concatenate([late] + others, 0)
    pair = swap(after(late, value), row_flip=0, feat_flip=1)
    others = [after(part, value) for part in early]
    partial_value = partial_scores(others, late, store, rows, tail)
    rest = jnp.concatenate(order[1::2], 1)
    return score_late(row, pair, rest, partial_value, index, value, row_groups)


def plain(slab_grads, basis, eigenvalues, store_rows, slab_index, *, row_groups, feat_groups):
    store_count = store_rows.shape[0]
    first_column = (lax.axis_index("rows") * feat_groups + lax.axis_index("feat")) * store_count
    columns = first_column + jnp.arange(store_count, dtype=jnp.int32)
    local_dirs = basis.shape[1]
    partial_value = jnp.dot(
        lax.all_gather(slab_grads, "rows", axis=0, tiled=True),
        basis,
        preferred_element_type=jnp.float32,
    )
    summed = lax.psum(partial_value, "feat")
    scales = lax.dynamic_slice_in_dim(
        eigenvalues, lax.axis_index("rows") * local_dirs, local_dirs, 0
    )
    whitened = (summed / (scales + DAMPING)).astype(jnp.bfloat16)
    gathered = lax.all_gather(whitened, "rows", axis=1, tiled=True)
    product = lax.dot_general(
        gathered, store_rows, CONTRACT_LAST, preferred_element_type=jnp.float32
    )
    return jnp.where(slab_index[:, None] == columns[None, :], jnp.zeros_like(product), product)


def solution(mesh):
    row_groups, feat_groups = mesh.shape["rows"], mesh.shape["feat"]
    powers = all(n > 1 and n & (n - 1) == 0 for n in (row_groups, feat_groups))

    def body(*args):
        sizes = dict(row_groups=row_groups, feat_groups=feat_groups)
        rows = args[0].shape[0]
        if not powers or rows < 96 or rows % 16 or args[1].shape[1] % 2:
            return plain(*args, **sizes)
        return shards(*args, **sizes)

    in_specs = (P("rows", "feat"), P("feat", "rows"), P(), P(("rows", "feat"), None), P())
    out_specs = P(None, ("rows", "feat"))
    return jax.shard_map(body, mesh=mesh, in_specs=in_specs, out_specs=out_specs, check_vma=False)
```
